32 devices in a mesh: snp: 8 (over z, y), samp: 4 (over x, core).
Axes of the slice: x: 2, y: 2, z: 4, core: 2. Of those that a mesh axis runs over, the one named last changes fastest.
Arguments:
- dosage: bfloat16 [5120, 8192], P('samp', 'snp'), may hold values from 0 to 2, as said below
- observed: int32 [5120, 8192], P('samp', 'snp'), may hold values 0 or 1
- band: int32 [8], replicated, may hold values from 1 to 2
Outputs:
- linkage: float32 [8192, 5120], P(('snp', 'samp'))
The draws below stay inside these ranges and needn't reach their ends.
Inputs may be any that keep to these rules, and one draw needn't show every extreme that they name: `dosage`: real-valued dosages.
All inputs are finite; a program needn't handle non-finite values. No bound on the sum of `observed` on one device may be relied on, other than what follows from the above.
Results may differ from the reference program's by a relative error of at most 0.00055.
Values may be sent and summed in bfloat16 or wider, within the bound.
A program may use at most 128 MiB of HBM per device.

```python
import jax
import jax.numpy as jnp
from jax import lax

B = 1024
NBLK = 8
NSNP = 8192
SAMPLES = 5120


def draw_dosage(key, part):
    keys = jax.random.split(key, 10)
    count = max(B // 4, 4)
    shape = (NBLK + 2, count)
    factors = jax.random.normal(keys[0], (SAMPLES, NBLK + 2, count), jnp.float32)
    starts = (jnp.arange(NBLK + 2, dtype=jnp.int32)[:, None] - 2) * B + jax.random.randint(keys[1], shape, 0, B)
    top = (2 * B).bit_length() - 1
    exponent = jax.random.randint(keys[2], shape, 4, top)
    powers = jnp.left_shift(jnp.ones_like(exponent), exponent)
    lengths = powers + jax.random.randint(keys[3], shape, 0, 1048576) % powers
    signs = (2 * jax.random.randint(keys[4], shape, 0, 2) - 1).astype(jnp.float32)

    def one_block(blk):
        near = lax.dynamic_slice_in_dim(factors, blk, 3, 1).reshape(SAMPLES, 3 * count)
        first = lax.dynamic_slice_in_dim(starts, blk, 3, 0).reshape(3 * count)
        span = lax.dynamic_slice_in_dim(lengths, blk, 3, 0).reshape(3 * count)
        sign = lax.dynamic_slice_in_dim(signs, blk, 3, 0).reshape(3 * count)
        column = blk * B + jnp.arange(B, dtype=jnp.int32)
        cover = (first[:, None] <= column[None, :]) & (column[None, :] < first[:, None] + span[:, None])
        loads = sign[:, None] * (0.5 + 0.5 * jax.random.normal(jax.random.fold_in(keys[5], blk), (3 * count, B), jnp.float32))
        loads = jnp.where(cover, loads, 0.0)
        scale = lax.rsqrt(jnp.sum(loads * loads, axis=0) + 0.25)
        return jnp.dot(near, loads) * scale[None, :]
    latent = lax.map(one_block, jnp.arange(NBLK, dtype=jnp.int32))
    latent = jnp.transpose(latent, (1, 0, 2)).reshape(SAMPLES, NSNP)
    latent = latent + 0.6 * jax.random.normal(keys[6], (SAMPLES, NSNP), jnp.float32)
    ramp = jnp.arange(SAMPLES, dtype=jnp.float32) / SAMPLES - 0.5
    tilt = jax.random.uniform(keys[7], (NSNP,), jnp.float32, -1.5, 1.5)
    slope = jax.random.uniform(keys[8], (NSNP,), jnp.float32, 0.6, 1.6)
    offset = 0.7 * jax.random.normal(keys[9], (NSNP,), jnp.float32)
    latent = latent + ramp[:, None] * tilt[None, :]
    return (2.0 * jax.nn.sigmoid(slope * latent + offset)).astype(jnp.bfloat16)


def plant(values, own_key, smallest, top_value):
    shape = values.shape
    index_at = [jax.random.randint(jax.random.fold_in(own_key, axis), (), 0, shape[axis]) for axis in range(len(shape))]
    values = values.at[tuple(index_at)].set(smallest)
    longest = shape.index(max(shape))
    index_at[longest] = (index_at[longest] + 1) % shape[longest]
    return values.at[tuple(index_at)].set(top_value)


def setup_inputs(seed: int = 0) -> dict:
    key_of = jax.random.split(jax.random.key(seed), 4)
    dosage = draw_dosage(jax.random.fold_in(key_of[3], 71), 0)
    observed = plant((jax.random.randint(key_of[1], (SAMPLES, NSNP), 0, 10) < 9).astype(jnp.int32), jax.random.fold_in(key_of[1], 1), 0, 1)
    band = plant(jax.random.randint(key_of[2], (NBLK,), 1, 3), jax.random.fold_in(key_of[2], 1), 1, 2).astype(jnp.int32)
    return {"dosage": dosage, "observed": observed, "band": band}


eps = 1e-05

def reference(dosage, observed, band):
    weight = observed.astype(jnp.float32)
    values = dosage.astype(jnp.float32)
    cnt = lax.optimization_barrier(jnp.sum(weight, axis=0))
    first = lax.optimization_barrier(jnp.sum(weight * values, axis=0))
    second = lax.optimization_barrier(jnp.sum(weight * values * values, axis=0))
    mean = first / cnt
    spread = second - first * mean
    zed = (weight * (values - mean) * lax.rsqrt(spread + eps * cnt)).astype(jnp.bfloat16)
    padded = jnp.pad(zed, ((0, 0), (2 * B, 2 * B)))
    offsets = jnp.arange(5, dtype=jnp.int32) - 2

    def one_block(blk):
        own = lax.dynamic_slice_in_dim(zed, blk * B, B, 1)
        near = lax.dynamic_slice_in_dim(padded, blk * B, 5 * B, 1)
        gram = jnp.dot(own.T, near, preferred_element_type=jnp.float32)
        other = blk + offsets
        inside = (other >= 0) & (other < NBLK)
        other_band = band[jnp.clip(other, 0, NBLK - 1)]
        keep = inside & (jnp.abs(offsets) <= jnp.minimum(band[blk], other_band))
        keep = jnp.where(keep, 1.0, 0.0).astype(jnp.float32)
        return (gram.reshape(B, 5, B) * keep[None, :, None]).reshape(B, 5 * B)
    result = lax.map(one_block, jnp.arange(NBLK, dtype=jnp.int32))
    return result.reshape(NSNP, 5 * B)
```

```python
import functools

import jax
import jax.numpy as jnp
from jax import lax
from jax.experimental import pallas as pl
from jax.experimental.pallas import tpu as pltpu
from jax.sharding import PartitionSpec as P

eps = 1e-05
MESH = pl.DeviceIdType.MESH
CHUNK = 256
TOP = 32767.0
RANGE = 2.0
CODE = TOP / RANGE**0.5


def offset_of(slot, e):
    return jnp.where(slot == 1, -e, jnp.where(slot == 2, -2 * e, jnp.where(slot == 3, 2 * e, jnp.where(slot == 4, e, 0))))


def encode(values):
    root = values * lax.rsqrt(jnp.maximum(jnp.abs(values), 1e-30)) * CODE
    code = jnp.round(jnp.clip(root, -TOP, TOP)).astype(jnp.int32)
    half = values.shape[0] // 2
    return lax.shift_left(code[:half], 16) | (code[half:] & 65535)


def decode(word):
    def value(code):
        f = code.astype(jnp.float32)
        return f * jnp.abs(f) * (1.0 / (CODE * CODE))

    return value(lax.shift_right_arithmetic(word, 16)), value(lax.shift_right_arithmetic(lax.shift_left(word, 16), 16))


def linkage_kernel(
    nblk, nsamp, nk, band_ref, dosage_ref, observed_ref, out_ref,
    dosages, marks, stats, zt, diag, part_out, part_in, diag_part_out, diag_part_in, diag_out, diag_in,
    dosage_sem, mark_sem, stat_send, stat_recv, z_send, z_recv, fwd_send, fwd_recv,
    part_send, part_recv, dpart_send, dpart_recv, diag_send, diag_recv,
):
    b = lax.axis_index("snp")
    s = lax.axis_index("samp")
    ngrp = nsamp // 2
    c = s % 2
    g = s // 2
    mate = s + 1 - 2 * c
    e = 2 * (b % 2) - 1
    width = nk * CHUNK
    rows = width // nsamp
    half = rows // 2

    def inside(block):
        return (block >= 0) & (block < nblk)

    def has(slot):
        return inside(b + offset_of(slot, e))

    npiece = nk + 1
    short = CHUNK // 2

    def columns(k):
        return pl.ds(pl.multiple_of(k * CHUNK, CHUNK), CHUNK)

    def chunk_at(slot, p):
        return jnp.where((slot < 2) | (p == 0), p, jnp.where(p == nk - 1, 1, p + 1))

    def place_of(slot, k):
        p = jnp.where((slot < 2) | (k == 0), k, jnp.where(k == 1, nk - 1, k - 1))
        return jnp.where(p == nk - 1, nk, p)

    def start_of(slot, p):
        return jnp.where(p < nk, chunk_at(slot, p) * CHUNK, chunk_at(slot, nk - 1) * CHUNK + short)

    def piece(slot, p, size):
        return pl.ds(pl.multiple_of(start_of(slot, p), short), size)

    def room(slot, start, size):
        return pl.ds(pl.multiple_of((offset_of(slot, e) + 2) * width + start, short), size)

    def load(k):
        part = pl.ds(k * CHUNK, CHUNK)
        return (
            pltpu.make_async_copy(dosage_ref.at[:, part], dosages.at[k], dosage_sem.at[k]),
            pltpu.make_async_copy(observed_ref.at[:, part], marks.at[k], mark_sem.at[k]),
        )

    for k in range(nk):
        for copy in load(k):
            copy.start()

    barrier = pltpu.get_barrier_semaphore()
    for j in range(1, nsamp):
        pl.semaphore_signal(barrier, inc=1, device_id=(b, (s + j) % nsamp), device_id_type=MESH)
    for slot in (1, 2, 3):
        @pl.when(has(slot))
        def _():
            pl.semaphore_signal(barrier, inc=1, device_id=(b + offset_of(slot, e), s), device_id_type=MESH)

    depth = dosages.shape[1]
    lanes = 128

    def tell(j, k):
        return pltpu.make_async_remote_copy(
            stats.at[s, k], stats.at[s, k], stat_send.at[j - 1, k], stat_recv.at[j - 1, k],
            device_id=(b, (s + j) % nsamp), device_id_type=MESH)

    def hear(j, k):
        other = (s + nsamp - j) % nsamp
        return pltpu.make_async_remote_copy(
            stats.at[other, k], stats.at[other, k], stat_send.at[j - 1, k], stat_recv.at[j - 1, k],
            device_id=(b, other), device_id_type=MESH)

    for k in range(nk):
        for copy in load(k):
            copy.wait()

        def add_rows(r, sums):
            at = pl.ds(pl.multiple_of(r * lanes, lanes), lanes)
            weight = marks[k, at, :].astype(jnp.float32)
            first = weight * dosages[k, at, :].astype(jnp.float32)
            second = first * dosages[k, at, :].astype(jnp.float32)
            return tuple(
                total + jnp.sum(term.reshape(lanes // 8, 8, CHUNK), axis=0)
                for total, term in zip(sums, (weight, first, second))
            )

        zero = jnp.zeros((8, CHUNK), jnp.float32)
        sums = lax.fori_loop(0, depth // lanes, add_rows, (zero, zero, zero))
        for q in range(3):
            stats[s, k, q : q + 1, :] = jnp.sum(sums[q], axis=0, keepdims=True)
        stats[s, k, 3:8, :] = jnp.zeros((5, CHUNK), jnp.float32)
        if k == 0:
            beside = [jnp.where(has(slot), 1, 0) for slot in (1, 2, 3)]
            pl.semaphore_wait(barrier, nsamp - 1 + sum(beside))
        for j in range(1, nsamp):
            tell(j, k).start()

    def direct(way, p, size):
        target = b + (-e, 2 * e, -2 * e)[way - 1]
        return target, pltpu.make_async_remote_copy(
            zt.at[0, c, piece(way, p, size)], zt.at[way, c, piece(way, p, size)], z_send.at[way, p], z_recv.at[way, p],
            device_id=(target, s), device_id_type=MESH)

    def arrival(slot, p, size):
        return pltpu.make_async_remote_copy(
            zt.at[slot, c, piece(slot, p, size)], zt.at[slot, c, piece(slot, p, size)], z_send.at[slot, p], z_recv.at[slot, p],
            device_id=(b, mate), device_id_type=MESH)

    def forward(slot, p, size):
        return pltpu.make_async_remote_copy(
            zt.at[slot, c, piece(slot, p, size)], zt.at[slot, c, piece(slot, p, size)], fwd_send.at[slot, p], fwd_recv.at[slot, p],
            device_id=(b, mate), device_id_type=MESH)

    def forward_in(slot, p, size):
        return pltpu.make_async_remote_copy(
            zt.at[slot, 1 - c, piece(slot, p, size)], zt.at[slot, 1 - c, piece(slot, p, size)],
            fwd_send.at[slot, p], fwd_recv.at[slot, p],
            device_id=(b, mate), device_id_type=MESH)

    sizes = [CHUNK] * (nk - 1) + [short, short]
    order = [0, *range(2, nk), 1]

    def send(way, p):
        target, copy = direct(way, p, sizes[p])

        @pl.when(inside(target))
        def _():
            copy.start()

    for k in range(nk):
        for j in range(1, nsamp):
            hear(j, k).wait_recv()
        part = stats[0, k]
        for other in range(1, nsamp):
            part = part + stats[other, k]
        cnt, first, second = part[0:1], part[1:2], part[2:3]
        mean = first / cnt
        scale = lax.rsqrt(second - first * mean + eps * cnt)

        def standardize(r, carry):
            at = pl.ds(pl.multiple_of(r * lanes, lanes), lanes)
            weight = marks[k, at, :].astype(jnp.float32)
            values = dosages[k, at, :].astype(jnp.float32)
            zed = (weight * (values - mean) * scale).astype(jnp.bfloat16)
            zt[0, c, columns(k), at] = zed.T
            return carry

        lax.fori_loop(0, depth // lanes, standardize, 0)
        for way in (1, 2, 3):
            done = range(k + 1)
            before = range(k)
            sequence = range(nk) if way == 1 else order
            def gone(chunks):
                n = 0
                while n < nk and sequence[n] in chunks:
                    n += 1
                return n
            for p in range(gone(before), gone(done)):
                send(way, p)
                if p == nk - 1:
                    send(way, nk)
        forward(0, k, CHUNK).start()

    def product(left, group, right, at):
        own_rows = pl.ds(pl.multiple_of((2 * group + c) * rows, rows), rows)
        both = [
            lax.dot_general(
                zt[left, h, own_rows, :], zt[right, h, at, :], (((1,), (1,)), ((), ())),
                preferred_element_type=jnp.float32)
            for h in range(2)
        ]
        return both[0] + both[1]

    def partial(i, j, size):
        return pltpu.make_async_remote_copy(
            part_out.at[i, j - 1, :, 0:size], part_in.at[i, j - 1, :, 0:size], part_send.at[i, j - 1], part_recv.at[i, j - 1],
            device_id=(b, 2 * ((g + j) % ngrp) + c), device_id_type=MESH)

    def multiply(slot, p, size, start):
        i = slot * npiece + p
        at = pl.ds(pl.multiple_of(start, short), size)
        for j in range(1, ngrp):
            part_out[i, j - 1, :, 0:size] = encode(product(0, (g + j) % ngrp, slot, at))
            partial(i, j, size).start()
        out_ref[:, room(slot, start, size)] = product(0, g, slot, at)

    def kept(slot):
        offset = offset_of(slot, e)
        inner = jnp.abs(offset) <= jnp.minimum(band_ref[b], band_ref[b + offset])
        return jnp.where(inner, 1.0, 0.0).astype(jnp.float32)

    def finish(slot, p, size, start):
        i = slot * npiece + p
        to = room(slot, start, size)
        upper, lower = out_ref[:half, to], out_ref[half:, to]
        for j in range(1, ngrp):
            partial(i, j, size).wait_recv()
            high, low = decode(part_in[i, j - 1, :, 0:size])
            upper, lower = upper + high, lower + low
        keep = kept(slot)
        out_ref[:half, to] = upper * keep
        out_ref[half:, to] = lower * keep

    makes = has(1) & has(2)

    def left_of(k):
        return jnp.where(k < nk // 2, 2, 1)

    def ready(group, k):
        left = left_of(k)
        return jnp.maximum(place_of(left, ((2 * group + c) * rows) // CHUNK), place_of(3 - left, k))

    def diag_partial(k, j):
        return pltpu.make_async_remote_copy(
            diag_part_out.at[k, j - 1], diag_part_in.at[k, j - 1], dpart_send.at[k, j - 1], dpart_recv.at[k, j - 1],
            device_id=(b, 2 * ((g + j) % ngrp) + c), device_id_type=MESH)

    def diag_final(k):
        return pltpu.make_async_remote_copy(
            diag_out.at[k], diag_in.at[k], diag_send.at[k], diag_recv.at[k],
            device_id=(jnp.where(k < nk // 2, b - 2 * e, b - e), s), device_id_type=MESH)

    def diag_multiply(t):
        def one(k, carry):
            left = left_of(k)
            for j in range(1, ngrp):
                group = (g + j) % ngrp

                @pl.when(ready(group, k) == t)
                def _():
                    diag_part_out[k, j - 1] = encode(product(left, group, 3 - left, columns(k)))
                    diag_partial(k, j).start()

            @pl.when(ready(g, k) == t)
            def _():
                diag[k] = product(left, g, 3 - left, columns(k))
            return carry

        lax.fori_loop(0, nk, one, 0)

    def diag_complete(t):
        def one(k, carry):
            @pl.when(ready(g, k) == t)
            def _():
                upper, lower = diag[k, :half, :], diag[k, half:, :]
                for j in range(1, ngrp):
                    diag_partial(k, j).wait_recv()
                    high, low = decode(diag_part_in[k, j - 1])
                    upper, lower = upper + high, lower + low
                diag_out[k] = encode(jnp.concatenate([upper, lower], axis=0))
                diag_final(k).start()
            return carry

        lax.fori_loop(0, nk, one, 0)

    for k in range(nk):
        forward_in(0, k, CHUNK).wait_recv()

    def own(k, carry):
        multiply(0, k, CHUNK, k * CHUNK)
        return carry

    lax.fori_loop(0, nk, own, 0)

    def nothing(slot, carry):
        @pl.when(jnp.logical_not(has(slot)))
        def _():
            def zeros(k, inner):
                out_ref[:, room(slot, k * CHUNK, CHUNK)] = jnp.zeros((rows, CHUNK), jnp.float32)
                return inner

            lax.fori_loop(0, nk, zeros, 0)
        return carry

    lax.fori_loop(1, 5, nothing, 0)

    def own_finish(k, carry):
        finish(0, k, CHUNK, k * CHUNK)
        return carry

    lax.fori_loop(0, nk, own_finish, 0)

    def each_slot(act):
        def one(slot, carry):
            @pl.when(has(slot))
            def _():
                act(slot)
            return carry

        lax.fori_loop(1, 4, one, 0)

    def finish_stage(p, size):
        each_slot(lambda slot: finish(slot, p, size, start_of(slot, p)))

    def stage(p, size):
        def receive(slot):
            arrival(slot, p, size).wait_recv()
            forward(slot, p, size).start()

        each_slot(receive)
        each_slot(lambda slot: forward_in(slot, p, size).wait_recv())

        @pl.when(makes)
        def _():
            diag_multiply(p)

        each_slot(lambda slot: multiply(slot, p, size, start_of(slot, p)))

    def full_stage(p, carry):
        stage(p, CHUNK)

        @pl.when(p > 0)
        def _():
            @pl.when(makes)
            def _():
                diag_complete(p - 1)
            finish_stage(p - 1, CHUNK)
        return carry

    lax.fori_loop(0, nk - 1, full_stage, 0)
    stage(nk - 1, short)

    @pl.when(makes)
    def _():
        diag_complete(nk - 2)
    finish_stage(nk - 2, CHUNK)
    stage(nk, short)

    @pl.when(makes)
    def _():
        diag_complete(nk)
    finish_stage(nk - 1, short)
    finish_stage(nk, short)

    @pl.when(has(4))
    def _():
        def one(k, carry):
            diag_final(k).wait_recv()
            high, low = decode(diag_in[k])
            keep = kept(4)
            out_ref[:half, room(4, k * CHUNK, CHUNK)] = high * keep
            out_ref[half:, room(4, k * CHUNK, CHUNK)] = low * keep
            return carry

        lax.fori_loop(0, nk, one, 0)

    def own_drain(k, carry):
        forward(0, k, CHUNK).wait_send()
        for j in range(1, ngrp):
            partial(k, j, CHUNK).wait_send()
        return carry

    lax.fori_loop(0, nk, own_drain, 0)
    for p in range(npiece):
        def drain(slot):
            forward(slot, p, sizes[p]).wait_send()
            for j in range(1, ngrp):
                partial(slot * npiece + p, j, sizes[p]).wait_send()

        each_slot(drain)

    @pl.when(makes)
    def _():
        def one(k, carry):
            for j in range(1, ngrp):
                diag_partial(k, j).wait_send()
            diag_final(k).wait_send()
            return carry

        lax.fori_loop(0, nk, one, 0)

    for j in range(1, nsamp):
        for k in range(nk):
            tell(j, k).wait_send()
    for p in range(npiece):
        for way in (1, 2, 3):
            target, copy = direct(way, p, sizes[p])

            @pl.when(inside(target))
            def _():
                copy.wait_send()


def on_device(nblk, nsamp, dosage, observed, band):
    depth, width = dosage.shape
    nk = width // CHUNK
    ngrp = nsamp // 2
    rows = width // nsamp
    npiece = nk + 1
    dma = pltpu.SemaphoreType.DMA
    coded = lambda *lead: pltpu.VMEM((*lead, rows // 2, CHUNK), jnp.int32)
    return pl.pallas_call(
        functools.partial(linkage_kernel, nblk, nsamp, nk),
        out_shape=pltpu.VMEM((rows, 5 * width), jnp.float32),
        in_specs=[
            pl.BlockSpec(memory_space=pltpu.SMEM),
            pl.BlockSpec(memory_space=pl.ANY),
            pl.BlockSpec(memory_space=pl.ANY),
        ],
        out_specs=pl.BlockSpec(memory_space=pltpu.VMEM),
        scratch_shapes=[
            pltpu.VMEM((nk, depth, CHUNK), jnp.bfloat16),
            pltpu.VMEM((nk, depth, CHUNK), jnp.int32),
            pltpu.VMEM((nsamp, nk, 8, CHUNK), jnp.float32),
            pltpu.VMEM((4, 2, width, depth), jnp.bfloat16),
            pltpu.VMEM((nk, rows, CHUNK), jnp.float32),
            coded(4 * npiece, ngrp - 1),
            coded(4 * npiece, ngrp - 1),
            coded(nk, ngrp - 1),
            coded(nk, ngrp - 1),
            coded(nk),
            coded(nk),
            dma((nk,)),
            dma((nk,)),
            dma((nsamp - 1, nk)),
            dma((nsamp - 1, nk)),
            dma((4, npiece)),
            dma((4, npiece)),
            dma((4, npiece)),
            dma((4, npiece)),
            dma((4 * npiece, ngrp - 1)),
            dma((4 * npiece, ngrp - 1)),
            dma((nk, ngrp - 1)),
            dma((nk, ngrp - 1)),
            dma((nk,)),
            dma((nk,)),
        ],
        compiler_params=pltpu.CompilerParams(
            collective_id=0, has_side_effects=True, vmem_limit_bytes=50000 * 1024
        ),
    )(band, dosage, observed)


def solution(mesh):
    return jax.shard_map(
        functools.partial(on_device, mesh.shape["snp"], mesh.shape["samp"]),
        mesh=mesh,
        in_specs=(P("samp", "snp"), P("samp", "snp"), P()),
        out_specs=P(("snp", "samp"), None),
        check_vma=False,
    )
```

```python
import functools

import jax
import jax.numpy as jnp
from jax import lax
from jax.experimental import pallas as pl
from jax.experimental.pallas import tpu as pltpu
from jax.sharding import PartitionSpec as P

eps = 1e-05
MESH = pl.DeviceIdType.MESH
CHUNK = 256
TOP = 32767.0
RANGE = 2.0
CODE = TOP / RANGE**0.5


def offset_of(slot, e):
    return jnp.where(slot == 1, -e, jnp.where(slot == 2, -2 * e, jnp.where(slot == 3, 2 * e, jnp.where(slot == 4, e, 0))))


def encode(values):
    root = values * lax.rsqrt(jnp.maximum(jnp.abs(values), 1e-30)) * CODE
    code = jnp.round(jnp.clip(root, -TOP, TOP)).astype(jnp.int32)
    half = values.shape[0] // 2
    return lax.shift_left(code[:half], 16) | (code[half:] & 65535)


def decode(word):
    def value(code):
        f = code.astype(jnp.float32)
        return f * jnp.abs(f) * (1.0 / (CODE * CODE))

    return value(lax.shift_right_arithmetic(word, 16)), value(lax.shift_right_arithmetic(lax.shift_left(word, 16), 16))


def linkage_kernel(
    nblk, nsamp, nk, band_ref, dosage_ref, observed_ref, out_ref,
    dosages, marks, stats, zt, diag, part_out, part_in, diag_part_out, diag_part_in, diag_out, diag_in,
    dosage_sem, mark_sem, stat_send, stat_recv, z_send, z_recv, fwd_send, fwd_recv,
    part_send, part_recv, dpart_send, dpart_recv, diag_send, diag_recv,
):
    b = lax.axis_index("snp")
    s = lax.axis_index("samp")
    ngrp = nsamp // 2
    c = s % 2
    g = s // 2
    mate = s + 1 - 2 * c
    e = 2 * (b % 2) - 1
    width = nk * CHUNK
    rows = width // nsamp
    half = rows // 2

    def inside(block):
        return (block >= 0) & (block < nblk)

    def has(slot):
        return inside(b + offset_of(slot, e))

    npiece = nk + 1
    short = CHUNK // 2

    def columns(k):
        return pl.ds(pl.multiple_of(k * CHUNK, CHUNK), CHUNK)

    def chunk_at(slot, p):
        return jnp.where((slot < 2) | (p == 0), p, jnp.where(p == nk - 1, 1, p + 1))

    def place_of(slot, k):
        p = jnp.where((slot < 2) | (k == 0), k, jnp.where(k == 1, nk - 1, k - 1))
        return jnp.where(p == nk - 1, nk, p)

    def start_of(slot, p):
        return jnp.where(p < nk, chunk_at(slot, p) * CHUNK, chunk_at(slot, nk - 1) * CHUNK + short)

    def piece(slot, p, size):
        return pl.ds(pl.multiple_of(start_of(slot, p), short), size)

    def room(slot, start, size):
        return pl.ds(pl.multiple_of((offset_of(slot, e) + 2) * width + start, short), size)

    def load(k):
        part = pl.ds(k * CHUNK, CHUNK)
        return (
            pltpu.make_async_copy(dosage_ref.at[:, part], dosages.at[k], dosage_sem.at[k]),
            pltpu.make_async_copy(observed_ref.at[:, part], marks.at[k], mark_sem.at[k]),
        )

    for k in range(nk):
        for copy in load(k):
            copy.start()

    barrier = pltpu.get_barrier_semaphore()
    for j in range(1, nsamp):
        pl.semaphore_signal(barrier, inc=1, device_id=(b, (s + j) % nsamp), device_id_type=MESH)
    for slot in (1, 2, 3):
        @pl.when(has(slot))
        def _():
            pl.semaphore_signal(barrier, inc=1, device_id=(b + offset_of(slot, e), s), device_id_type=MESH)

    depth = dosages.shape[1]
    lanes = 128

    def tell(j, k):
        return pltpu.make_async_remote_copy(
            stats.at[s, k], stats.at[s, k], stat_send.at[j - 1, k], stat_recv.at[j - 1, k],
            device_id=(b, (s + j) % nsamp), device_id_type=MESH)

    def hear(j, k):
        other = (s + nsamp - j) % nsamp
        return pltpu.make_async_remote_copy(
            stats.at[other, k], stats.at[other, k], stat_send.at[j - 1, k], stat_recv.at[j - 1, k],
            device_id=(b, other), device_id_type=MESH)

    for k in range(nk):
        for copy in load(k):
            copy.wait()

        def add_rows(r, sums):
            at = pl.ds(pl.multiple_of(r * lanes, lanes), lanes)
            weight = marks[k, at, :].astype(jnp.float32)
            first = weight * dosages[k, at, :].astype(jnp.float32)
            second = first * dosages[k, at, :].astype(jnp.float32)
            return tuple(
                total + jnp.sum(term.reshape(lanes // 8, 8, CHUNK), axis=0)
                for total, term in zip(sums, (weight, first, second))
            )

        zero = jnp.zeros((8, CHUNK), jnp.float32)
        sums = lax.fori_loop(0, depth // lanes, add_rows, (zero, zero, zero))
        for q in range(3):
            stats[s, k, q : q + 1, :] = jnp.sum(sums[q], axis=0, keepdims=True)
        stats[s, k, 3:8, :] = jnp.zeros((5, CHUNK), jnp.float32)
        if k == 0:
            beside = [jnp.where(has(slot), 1, 0) for slot in (1, 2, 3)]
            pl.semaphore_wait(barrier, nsamp - 1 + sum(beside))
        for j in range(1, nsamp):
            tell(j, k).start()

    def direct(way, p, size):
        target = b + (-e, 2 * e, -2 * e)[way - 1]
        return target, pltpu.make_async_remote_copy(
            zt.at[0, c, piece(way, p, size)], zt.at[way, c, piece(way, p, size)], z_send.at[way, p], z_recv.at[way, p],
            device_id=(target, s), device_id_type=MESH)

    def arrival(slot, p, size):
        return pltpu.make_async_remote_copy(
            zt.at[slot, c, piece(slot, p, size)], zt.at[slot, c, piece(slot, p, size)], z_send.at[slot, p], z_recv.at[slot, p],
            device_id=(b, mate), device_id_type=MESH)

    def forward(slot, p, size):
        return pltpu.make_async_remote_copy(
            zt.at[slot, c, piece(slot, p, size)], zt.at[slot, c, piece(slot, p, size)], fwd_send.at[slot, p], fwd_recv.at[slot, p],
            device_id=(b, mate), device_id_type=MESH)

    def forward_in(slot, p, size):
        return pltpu.make_async_remote_copy(
            zt.at[slot, 1 - c, piece(slot, p, size)], zt.at[slot, 1 - c, piece(slot, p, size)],
            fwd_send.at[slot, p], fwd_recv.at[slot, p],
            device_id=(b, mate), device_id_type=MESH)

    sizes = [CHUNK] * (nk - 1) + [short, short]
    order = [0, *range(2, nk), 1]

    def send(way, p):
        target, copy = direct(way, p, sizes[p])

        @pl.when(inside(target))
        def _():
            copy.start()

    for k in range(nk):
        for j in range(1, nsamp):
            hear(j, k).wait_recv()
        part = stats[0, k]
        for other in range(1, nsamp):
            part = part + stats[other, k]
        cnt, first, second = part[0:1], part[1:2], part[2:3]
        mean = first / cnt
        scale = lax.rsqrt(second - first * mean + eps * cnt)

        def standardize(r, carry):
            at = pl.ds(pl.multiple_of(r * lanes, lanes), lanes)
            weight = marks[k, at, :].astype(jnp.float32)
            values = dosages[k, at, :].astype(jnp.float32)
            zed = (weight * (values - mean) * scale).astype(jnp.bfloat16)
            zt[0, c, columns(k), at] = zed.T
            return carry

        lax.fori_loop(0, depth // lanes, standardize, 0)
        for way in (1, 2, 3):
            done = range(k + 1)
            before = range(k)
            sequence = range(nk) if way == 1 else order
            def gone(chunks):
                n = 0
                while n < nk and sequence[n] in chunks:
                    n += 1
                return n
            for p in range(gone(before), gone(done)):
                send(way, p)
                if p == nk - 1:
                    send(way, nk)
        forward(0, k, CHUNK).start()

    def product(left, group, right, at, low=0, size=rows):
        own_rows = pl.ds(pl.multiple_of((2 * group + c) * rows + low, size), size)
        both = [
            lax.dot_general(
                zt[left, h, own_rows, :], zt[right, h, at, :], (((1,), (1,)), ((), ())),
                preferred_element_type=jnp.float32)
            for h in range(2)
        ]
        return both[0] + both[1]

    def partial(i, j, size):
        return pltpu.make_async_remote_copy(
            part_out.at[i, j - 1, :, 0:size], part_in.at[i, j - 1, :, 0:size], part_send.at[i, j - 1], part_recv.at[i, j - 1],
            device_id=(b, 2 * ((g + j) % ngrp) + c), device_id_type=MESH)

    def multiply(slot, p, size, start):
        i = slot * npiece + p
        at = pl.ds(pl.multiple_of(start, short), size)
        for j in range(1, ngrp):
            part_out[i, j - 1, :, 0:size] = encode(product(0, (g + j) % ngrp, slot, at))
            partial(i, j, size).start()
        out_ref[:, room(slot, start, size)] = product(0, g, slot, at)

    def kept(slot):
        offset = offset_of(slot, e)
        inner = jnp.abs(offset) <= jnp.minimum(band_ref[b], band_ref[b + offset])
        return jnp.where(inner, 1.0, 0.0).astype(jnp.float32)

    def finish(slot, p, size, start):
        i = slot * npiece + p
        to = room(slot, start, size)
        upper, lower = out_ref[:half, to], out_ref[half:, to]
        for j in range(1, ngrp):
            partial(i, j, size).wait_recv()
            high, low = decode(part_in[i, j - 1, :, 0:size])
            upper, lower = upper + high, lower + low
        keep = kept(slot)
        out_ref[:half, to] = upper * keep
        out_ref[half:, to] = lower * keep

    makes = has(1) & has(2)

    quarter = half // 2

    def left_of(k):
        return jnp.where(k < nk // 2, 2, 1)

    def ready(group, u):
        k = u // 2
        left = left_of(k)
        first_row = (2 * group + c) * rows + (u % 2) * half
        place = place_of(left, first_row // CHUNK)
        place = jnp.where(place == nk, nk - 1 + (first_row % CHUNK) // short, place)
        return jnp.maximum(place, place_of(3 - left, k))

    def diag_partial(u, j):
        return pltpu.make_async_remote_copy(
            diag_part_out.at[u, j - 1], diag_part_in.at[u, j - 1], dpart_send.at[u, j - 1], dpart_recv.at[u, j - 1],
            device_id=(b, 2 * ((g + j) % ngrp) + c), device_id_type=MESH)

    def diag_final(u):
        return pltpu.make_async_remote_copy(
            diag_out.at[u], diag_in.at[u], diag_send.at[u], diag_recv.at[u],
            device_id=(jnp.where(u < nk, b - 2 * e, b - e), s), device_id_type=MESH)

    def diag_product(group, u):
        left = left_of(u // 2)
        return product(left, group, 3 - left, columns(u // 2), (u % 2) * half, half)

    def each_unit(group, p, act):
        def one(u, carry):
            @pl.when(ready(group, u) == p)
            def _():
                act(u)
            return carry

        lax.fori_loop(0, 2 * nk, one, 0)

    def diag_multiply(p):
        for j in range(1, ngrp):
            group = (g + j) % ngrp

            def away(u):
                diag_part_out[u, j - 1] = encode(diag_product(group, u))
                diag_partial(u, j).start()

            each_unit(group, p, away)

        def here(u):
            diag[u] = diag_product(g, u)

        each_unit(g, p, here)

    def diag_complete(p):
        def act(u):
            upper, lower = diag[u, :quarter, :], diag[u, quarter:, :]
            for j in range(1, ngrp):
                diag_partial(u, j).wait_recv()
                high, low = decode(diag_part_in[u, j - 1])
                upper, lower = upper + high, lower + low
            diag_out[u] = encode(jnp.concatenate([upper, lower], axis=0))
            diag_final(u).start()

        each_unit(g, p, act)

    def diag_receive(p):
        def act(u):
            diag_final(u).wait_recv()
            high, low = decode(diag_in[u])
            keep = kept(4)
            to = room(4, (u // 2) * CHUNK, CHUNK)
            row = (u % 2) * half
            out_ref[pl.ds(pl.multiple_of(row, quarter), quarter), to] = high * keep
            out_ref[pl.ds(pl.multiple_of(row + quarter, quarter), quarter), to] = low * keep

        each_unit(g, p, act)

    for k in range(nk):
        forward_in(0, k, CHUNK).wait_recv()

    def own(k, carry):
        multiply(0, k, CHUNK, k * CHUNK)
        return carry

    lax.fori_loop(0, nk, own, 0)

    def nothing(slot, carry):
        @pl.when(jnp.logical_not(has(slot)))
        def _():
            def zeros(k, inner):
                out_ref[:, room(slot, k * CHUNK, CHUNK)] = jnp.zeros((rows, CHUNK), jnp.float32)
                return inner

            lax.fori_loop(0, nk, zeros, 0)
        return carry

    lax.fori_loop(1, 5, nothing, 0)

    def own_finish(k, carry):
        finish(0, k, CHUNK, k * CHUNK)
        return carry

    lax.fori_loop(0, nk, own_finish, 0)

    def each_slot(act):
        def one(slot, carry):
            @pl.when(has(slot))
            def _():
                act(slot)
            return carry

        lax.fori_loop(1, 4, one, 0)

    def finish_stage(p, size):
        each_slot(lambda slot: finish(slot, p, size, start_of(slot, p)))

    def stage(p, size):
        def receive(slot):
            arrival(slot, p, size).wait_recv()
            forward(slot, p, size).start()

        @pl.when(has(2))
        def _():
            receive(2)
            forward_in(2, p, size).wait_recv()
            multiply(2, p, size, start_of(2, p))

        def others(act):
            def one(n, carry):
                slot = 1 + 2 * n

                @pl.when(has(slot))
                def _():
                    act(slot)
                return carry

            lax.fori_loop(0, 2, one, 0)

        others(receive)

        @pl.when(has(1))
        def _():
            forward_in(1, p, size).wait_recv()

        @pl.when(makes)
        def _():
            diag_multiply(p)

        def rest(slot):
            @pl.when(slot == 3)
            def _():
                forward_in(3, p, size).wait_recv()
            multiply(slot, p, size, start_of(slot, p))

        others(rest)

    def full_stage(p, carry):
        stage(p, CHUNK)

        @pl.when(p > 0)
        def _():
            @pl.when(makes)
            def _():
                diag_complete(p - 1)
            finish_stage(p - 1, CHUNK)
        return carry

    lax.fori_loop(0, nk - 1, full_stage, 0)
    stage(nk - 1, short)

    @pl.when(makes)
    def _():
        diag_complete(nk - 2)
    finish_stage(nk - 2, CHUNK)

    def early(p, carry):
        diag_receive(p)
        return carry

    @pl.when(has(4))
    def _():
        lax.fori_loop(0, nk - 2, early, 0)
    stage(nk, short)

    @pl.when(makes)
    def _():
        diag_complete(nk - 1)
    finish_stage(nk - 1, short)

    @pl.when(makes)
    def _():
        diag_complete(nk)

    @pl.when(has(4))
    def _():
        diag_receive(nk - 2)
    finish_stage(nk, short)

    @pl.when(has(4))
    def _():
        diag_receive(nk - 1)
        diag_receive(nk)

    def own_drain(k, carry):
        forward(0, k, CHUNK).wait_send()
        for j in range(1, ngrp):
            partial(k, j, CHUNK).wait_send()
        return carry

    lax.fori_loop(0, nk, own_drain, 0)
    for p in range(npiece):
        def drain(slot):
            forward(slot, p, sizes[p]).wait_send()
            for j in range(1, ngrp):
                partial(slot * npiece + p, j, sizes[p]).wait_send()

        each_slot(drain)

    @pl.when(makes)
    def _():
        def one(u, carry):
            for j in range(1, ngrp):
                diag_partial(u, j).wait_send()
            diag_final(u).wait_send()
            return carry

        lax.fori_loop(0, 2 * nk, one, 0)

    for j in range(1, nsamp):
        for k in range(nk):
            tell(j, k).wait_send()
    for p in range(npiece):
        for way in (1, 2, 3):
            target, copy = direct(way, p, sizes[p])

            @pl.when(inside(target))
            def _():
                copy.wait_send()


def on_device(nblk, nsamp, dosage, observed, band):
    depth, width = dosage.shape
    nk = width // CHUNK
    ngrp = nsamp // 2
    rows = width // nsamp
    npiece = nk + 1
    dma = pltpu.SemaphoreType.DMA
    coded = lambda *lead: pltpu.VMEM((*lead, CHUNK), jnp.int32)
    return pl.pallas_call(
        functools.partial(linkage_kernel, nblk, nsamp, nk),
        out_shape=pltpu.VMEM((rows, 5 * width), jnp.float32),
        in_specs=[
            pl.BlockSpec(memory_space=pltpu.SMEM),
            pl.BlockSpec(memory_space=pl.ANY),
            pl.BlockSpec(memory_space=pl.ANY),
        ],
        out_specs=pl.BlockSpec(memory_space=pltpu.VMEM),
        scratch_shapes=[
            pltpu.VMEM((nk, depth, CHUNK), jnp.bfloat16),
            pltpu.VMEM((nk, depth, CHUNK), jnp.int32),
            pltpu.VMEM((nsamp, nk, 8, CHUNK), jnp.float32),
            pltpu.VMEM((4, 2, width, depth), jnp.bfloat16),
            pltpu.VMEM((2 * nk, rows // 2, CHUNK), jnp.float32),
            coded(4 * npiece, ngrp - 1, rows // 2),
            coded(4 * npiece, ngrp - 1, rows // 2),
            coded(2 * nk, ngrp - 1, rows // 4),
            coded(2 * nk, ngrp - 1, rows // 4),
            coded(2 * nk, rows // 4),
            coded(2 * nk, rows // 4),
            dma((nk,)),
            dma((nk,)),
            dma((nsamp - 1, nk)),
            dma((nsamp - 1, nk)),
            dma((4, npiece)),
            dma((4, npiece)),
            dma((4, npiece)),
            dma((4, npiece)),
            dma((4 * npiece, ngrp - 1)),
            dma((4 * npiece, ngrp - 1)),
            dma((2 * nk, ngrp - 1)),
            dma((2 * nk, ngrp - 1)),
            dma((2 * nk,)),
            dma((2 * nk,)),
        ],
        compiler_params=pltpu.CompilerParams(
            collective_id=0, has_side_effects=True, vmem_limit_bytes=59000 * 1024
        ),
    )(band, dosage, observed)


def solution(mesh):
    return jax.shard_map(
        functools.partial(on_device, mesh.shape["snp"], mesh.shape["samp"]),
        mesh=mesh,
        in_specs=(P("samp", "snp"), P("samp", "snp"), P()),
        out_specs=P(("snp", "samp"), None),
        check_vma=False,
    )
```

```python
import functools

import jax
import jax.numpy as jnp
from jax import lax
from jax.experimental import pallas as pl
from jax.experimental.pallas import tpu as pltpu
from jax.sharding import PartitionSpec as P

eps = 1e-05
MESH = pl.DeviceIdType.MESH
CHUNK = 256
TOP = 32767.0
RANGE = 2.0
CODE = TOP / RANGE**0.5


def offset_of(slot, e):
    return jnp.where(slot == 1, -e, jnp.where(slot == 2, -2 * e, jnp.where(slot == 3, 2 * e, jnp.where(slot == 4, e, 0))))


def encode(values):
    root = values * lax.rsqrt(jnp.maximum(jnp.abs(values), 1e-30)) * CODE
    code = jnp.round(jnp.clip(root, -TOP, TOP)).astype(jnp.int32)
    half = values.shape[0] // 2
    return lax.shift_left(code[:half], 16) | (code[half:] & 65535)


def decode(word):
    def value(code):
        f = code.astype(jnp.float32)
        return f * jnp.abs(f) * (1.0 / (CODE * CODE))

    return value(lax.shift_right_arithmetic(word, 16)), value(lax.shift_right_arithmetic(lax.shift_left(word, 16), 16))


def linkage_kernel(
    nblk, nsamp, nk, band_ref, dosage_ref, observed_ref, out_ref,
    dosages, marks, stats, zt, diag, part_out, part_in, diag_part_out, diag_part_in, diag_out, diag_in,
    dosage_sem, mark_sem, stat_send, stat_recv, z_send, z_recv, fwd_send, fwd_recv,
    part_send, part_recv, dpart_send, dpart_recv, diag_send, diag_recv,
):
    b = lax.axis_index("snp")
    s = lax.axis_index("samp")
    ngrp = nsamp // 2
    c = s % 2
    g = s // 2
    mate = s + 1 - 2 * c
    e = 2 * (b % 2) - 1
    width = nk * CHUNK
    rows = width // nsamp
    half = rows // 2

    def inside(block):
        return (block >= 0) & (block < nblk)

    def has(slot):
        return inside(b + offset_of(slot, e))

    npiece = nk + 1
    short = CHUNK // 2

    def columns(k):
        return pl.ds(pl.multiple_of(k * CHUNK, CHUNK), CHUNK)

    def chunk_at(slot, p):
        return jnp.where((slot < 2) | (p == 0), p, jnp.where(p == nk - 1, 1, p + 1))

    def place_of(slot, k):
        p = jnp.where((slot < 2) | (k == 0), k, jnp.where(k == 1, nk - 1, k - 1))
        return jnp.where(p == nk - 1, nk, p)

    def start_of(slot, p):
        return jnp.where(p < nk, chunk_at(slot, p) * CHUNK, chunk_at(slot, nk - 1) * CHUNK + short)

    def piece(slot, p, size):
        return pl.ds(pl.multiple_of(start_of(slot, p), short), size)

    def room(slot, start, size):
        return pl.ds(pl.multiple_of((offset_of(slot, e) + 2) * width + start, short), size)

    def load(k):
        part = pl.ds(k * CHUNK, CHUNK)
        return (
            pltpu.make_async_copy(dosage_ref.at[:, part], dosages.at[k], dosage_sem.at[k]),
            pltpu.make_async_copy(observed_ref.at[:, part], marks.at[k], mark_sem.at[k]),
        )

    for k in range(nk):
        for copy in load(k):
            copy.start()

    barrier = pltpu.get_barrier_semaphore()
    for j in range(1, nsamp):
        pl.semaphore_signal(barrier, inc=1, device_id=(b, (s + j) % nsamp), device_id_type=MESH)
    for slot in (1, 2, 3):
        @pl.when(has(slot))
        def _():
            pl.semaphore_signal(barrier, inc=1, device_id=(b + offset_of(slot, e), s), device_id_type=MESH)

    depth = dosages.shape[1]
    lanes = 128

    def tell(j, k):
        return pltpu.make_async_remote_copy(
            stats.at[s, k], stats.at[s, k], stat_send.at[j - 1, k], stat_recv.at[j - 1, k],
            device_id=(b, (s + j) % nsamp), device_id_type=MESH)

    def hear(j, k):
        other = (s + nsamp - j) % nsamp
        return pltpu.make_async_remote_copy(
            stats.at[other, k], stats.at[other, k], stat_send.at[j - 1, k], stat_recv.at[j - 1, k],
            device_id=(b, other), device_id_type=MESH)

    def gather(k):
        for copy in load(k):
            copy.wait()

        def add_rows(r, sums):
            at = pl.ds(pl.multiple_of(r * lanes, lanes), lanes)
            weight = marks[k, at, :].astype(jnp.float32)
            first = weight * dosages[k, at, :].astype(jnp.float32)
            second = first * dosages[k, at, :].astype(jnp.float32)
            return tuple(
                total + jnp.sum(term.reshape(lanes // 8, 8, CHUNK), axis=0)
                for total, term in zip(sums, (weight, first, second))
            )

        zero = jnp.zeros((8, CHUNK), jnp.float32)
        sums = lax.fori_loop(0, depth // lanes, add_rows, (zero, zero, zero))
        for q in range(3):
            stats[s, k, q : q + 1, :] = jnp.sum(sums[q], axis=0, keepdims=True)
        stats[s, k, 3:8, :] = jnp.zeros((5, CHUNK), jnp.float32)
        if k == 0:
            beside = [jnp.where(has(slot), 1, 0) for slot in (1, 2, 3)]
            pl.semaphore_wait(barrier, nsamp - 1 + sum(beside))
        for j in range(1, nsamp):
            tell(j, k).start()

    def direct(way, p, size):
        target = b + (-e, 2 * e, -2 * e)[way - 1]
        return target, pltpu.make_async_remote_copy(
            zt.at[0, c, piece(way, p, size)], zt.at[way, c, piece(way, p, size)], z_send.at[way, p], z_recv.at[way, p],
            device_id=(target, s), device_id_type=MESH)

    def arrival(slot, p, size):
        return pltpu.make_async_remote_copy(
            zt.at[slot, c, piece(slot, p, size)], zt.at[slot, c, piece(slot, p, size)], z_send.at[slot, p], z_recv.at[slot, p],
            device_id=(b, mate), device_id_type=MESH)

    def forward(slot, p, size):
        return pltpu.make_async_remote_copy(
            zt.at[slot, c, piece(slot, p, size)], zt.at[slot, c, piece(slot, p, size)], fwd_send.at[slot, p], fwd_recv.at[slot, p],
            device_id=(b, mate), device_id_type=MESH)

    def forward_in(slot, p, size):
        return pltpu.make_async_remote_copy(
            zt.at[slot, 1 - c, piece(slot, p, size)], zt.at[slot, 1 - c, piece(slot, p, size)],
            fwd_send.at[slot, p], fwd_recv.at[slot, p],
            device_id=(b, mate), device_id_type=MESH)

    sizes = [CHUNK] * (nk - 1) + [short, short]
    order = [0, *range(2, nk), 1]

    def send(way, p):
        target, copy = direct(way, p, sizes[p])

        @pl.when(inside(target))
        def _():
            copy.start()

    def spread(k):
        for j in range(1, nsamp):
            hear(j, k).wait_recv()
        part = stats[0, k]
        for other in range(1, nsamp):
            part = part + stats[other, k]
        cnt, first, second = part[0:1], part[1:2], part[2:3]
        mean = first / cnt
        scale = lax.rsqrt(second - first * mean + eps * cnt)

        def standardize(r, carry):
            at = pl.ds(pl.multiple_of(r * lanes, lanes), lanes)
            weight = marks[k, at, :].astype(jnp.float32)
            values = dosages[k, at, :].astype(jnp.float32)
            zed = (weight * (values - mean) * scale).astype(jnp.bfloat16)
            zt[0, c, columns(k), at] = zed.T
            return carry

        lax.fori_loop(0, depth // lanes, standardize, 0)
        for way in (1, 2, 3):
            done = range(k + 1)
            before = range(k)
            sequence = range(nk) if way == 1 else order
            def gone(chunks):
                n = 0
                while n < nk and sequence[n] in chunks:
                    n += 1
                return n
            for p in range(gone(before), gone(done)):
                send(way, p)
                if p == nk - 1:
                    send(way, nk)
        forward(0, k, CHUNK).start()

    gather(0)
    for k in range(nk):
        if k + 1 < nk:
            gather(k + 1)
        spread(k)

    def product(left, group, right, at):
        own_rows = pl.ds(pl.multiple_of((2 * group + c) * rows, rows), rows)
        both = [
            lax.dot_general(
                zt[left, h, own_rows, :], zt[right, h, at, :], (((1,), (1,)), ((), ())),
                preferred_element_type=jnp.float32)
            for h in range(2)
        ]
        return both[0] + both[1]

    def partial(i, j, size):
        return pltpu.make_async_remote_copy(
            part_out.at[i, j - 1, :, 0:size], part_in.at[i, j - 1, :, 0:size], part_send.at[i, j - 1], part_recv.at[i, j - 1],
            device_id=(b, 2 * ((g + j) % ngrp) + c), device_id_type=MESH)

    def multiply_away(slot, p, size, start):
        i = slot * npiece + p
        at = pl.ds(pl.multiple_of(start, short), size)
        for j in range(1, ngrp):
            part_out[i, j - 1, :, 0:size] = encode(product(0, (g + j) % ngrp, slot, at))
            partial(i, j, size).start()

    def multiply_here(slot, size, start):
        at = pl.ds(pl.multiple_of(start, short), size)
        out_ref[:, room(slot, start, size)] = product(0, g, slot, at)

    def multiply(slot, p, size, start):
        multiply_away(slot, p, size, start)
        multiply_here(slot, size, start)

    def kept(slot):
        offset = offset_of(slot, e)
        inner = jnp.abs(offset) <= jnp.minimum(band_ref[b], band_ref[b + offset])
        return jnp.where(inner, 1.0, 0.0).astype(jnp.float32)

    def finish(slot, p, size, start):
        i = slot * npiece + p
        to = room(slot, start, size)
        upper, lower = out_ref[:half, to], out_ref[half:, to]
        for j in range(1, ngrp):
            partial(i, j, size).wait_recv()
            high, low = decode(part_in[i, j - 1, :, 0:size])
            upper, lower = upper + high, lower + low
        keep = kept(slot)
        out_ref[:half, to] = upper * keep
        out_ref[half:, to] = lower * keep

    makes = has(1) & has(2)


    def left_of(group, k):
        j = ((2 * group + c) * rows) // CHUNK
        return jnp.where(jnp.where((j == 0) | (j == nk - 1), k != nk - 1, k == 1), 2, 1)

    def ready(group, k):
        left = left_of(group, k)
        return jnp.maximum(place_of(left, ((2 * group + c) * rows) // CHUNK), place_of(3 - left, k))

    def diag_partial(u, j):
        return pltpu.make_async_remote_copy(
            diag_part_out.at[u, j - 1], diag_part_in.at[u, j - 1], dpart_send.at[u, j - 1], dpart_recv.at[u, j - 1],
            device_id=(b, 2 * ((g + j) % ngrp) + c), device_id_type=MESH)

    def diag_final(u):
        return pltpu.make_async_remote_copy(
            diag_out.at[u], diag_in.at[u], diag_send.at[u], diag_recv.at[u],
            device_id=(b - e * left_of(g, u), s), device_id_type=MESH)

    def diag_product(group, u):
        left = left_of(group, u)
        return product(left, group, 3 - left, columns(u))

    def each_unit(group, p, act):
        def one(u, carry):
            @pl.when(ready(group, u) == p)
            def _():
                act(u)
            return carry

        lax.fori_loop(0, nk, one, 0)

    def diag_away(p):
        for j in range(1, ngrp):
            group = (g + j) % ngrp

            def away(u):
                diag_part_out[u, j - 1] = encode(diag_product(group, u))
                diag_partial(u, j).start()

            each_unit(group, p, away)

    def diag_here(p):
        def here(u):
            diag[u] = diag_product(g, u)

        each_unit(g, p, here)

    def diag_complete(p):
        def act(u):
            upper, lower = diag[u, :half, :], diag[u, half:, :]
            for j in range(1, ngrp):
                diag_partial(u, j).wait_recv()
                high, low = decode(diag_part_in[u, j - 1])
                upper, lower = upper + high, lower + low
            diag_out[u] = encode(jnp.concatenate([upper, lower], axis=0))

        each_unit(g, p, act)

    def deliver(p):
        each_unit(g, p, lambda u: diag_final(u).start())

    def each_place(act):
        def one(p, carry):
            act(p)
            return carry

        lax.fori_loop(0, nk - 1, one, 0)

    def diag_receive(p):
        def act(u):
            diag_final(u).wait_recv()
            high, low = decode(diag_in[u])
            keep = kept(4)
            to = room(4, u * CHUNK, CHUNK)
            out_ref[:half, to] = high * keep
            out_ref[half:, to] = low * keep

        each_unit(g, p, act)

    for k in range(nk):
        forward_in(0, k, CHUNK).wait_recv()

    def own(k, carry):
        multiply(0, k, CHUNK, k * CHUNK)
        return carry

    lax.fori_loop(0, nk, own, 0)

    def nothing(slot, carry):
        @pl.when(jnp.logical_not(has(slot)))
        def _():
            def zeros(k, inner):
                out_ref[:, room(slot, k * CHUNK, CHUNK)] = jnp.zeros((rows, CHUNK), jnp.float32)
                return inner

            lax.fori_loop(0, nk, zeros, 0)
        return carry

    lax.fori_loop(1, 5, nothing, 0)

    def own_finish(k, carry):
        finish(0, k, CHUNK, k * CHUNK)
        return carry

    lax.fori_loop(0, nk, own_finish, 0)

    def each_slot(act):
        def one(slot, carry):
            @pl.when(has(slot))
            def _():
                act(slot)
            return carry

        lax.fori_loop(1, 4, one, 0)

    def finish_stage(p, size):
        each_slot(lambda slot: finish(slot, p, size, start_of(slot, p)))

    def stage(p, size, last=False):
        def receive(slot):
            arrival(slot, p, size).wait_recv()
            forward(slot, p, size).start()

        each_slot(receive)
        each_slot(lambda slot: forward_in(slot, p, size).wait_recv())

        @pl.when(makes)
        def _():
            if last:
                each_place(deliver)
            diag_away(p)
            diag_here(p)

        if last:
            each_slot(lambda slot: multiply_away(slot, p, size, start_of(slot, p)))
            each_slot(lambda slot: multiply_here(slot, size, start_of(slot, p)))
        else:
            each_slot(lambda slot: multiply(slot, p, size, start_of(slot, p)))

    def full_stage(p, carry):
        stage(p, CHUNK)

        @pl.when(p > 0)
        def _():
            @pl.when(makes)
            def _():
                diag_complete(p - 1)
            finish_stage(p - 1, CHUNK)
        return carry

    lax.fori_loop(0, nk - 1, full_stage, 0)
    stage(nk - 1, short)

    @pl.when(makes)
    def _():
        diag_complete(nk - 2)
    finish_stage(nk - 2, CHUNK)

    stage(nk, short, last=True)

    @pl.when(makes)
    def _():
        diag_complete(nk)
        deliver(nk)
    finish_stage(nk - 1, short)
    finish_stage(nk, short)

    @pl.when(has(4))
    def _():
        each_place(diag_receive)
        diag_receive(nk)

    def own_drain(k, carry):
        forward(0, k, CHUNK).wait_send()
        for j in range(1, ngrp):
            partial(k, j, CHUNK).wait_send()
        return carry

    lax.fori_loop(0, nk, own_drain, 0)
    for p in range(npiece):
        def drain(slot):
            forward(slot, p, sizes[p]).wait_send()
            for j in range(1, ngrp):
                partial(slot * npiece + p, j, sizes[p]).wait_send()

        each_slot(drain)

    @pl.when(makes)
    def _():
        def one(u, carry):
            for j in range(1, ngrp):
                diag_partial(u, j).wait_send()
            diag_final(u).wait_send()
            return carry

        lax.fori_loop(0, nk, one, 0)

    for j in range(1, nsamp):
        for k in range(nk):
            tell(j, k).wait_send()
    for p in range(npiece):
        for way in (1, 2, 3):
            target, copy = direct(way, p, sizes[p])

            @pl.when(inside(target))
            def _():
                copy.wait_send()


def on_device(nblk, nsamp, dosage, observed, band):
    depth, width = dosage.shape
    nk = width // CHUNK
    ngrp = nsamp // 2
    rows = width // nsamp
    npiece = nk + 1
    dma = pltpu.SemaphoreType.DMA
    coded = lambda *lead: pltpu.VMEM((*lead, CHUNK), jnp.int32)
    return pl.pallas_call(
        functools.partial(linkage_kernel, nblk, nsamp, nk),
        out_shape=pltpu.VMEM((rows, 5 * width), jnp.float32),
        in_specs=[
            pl.BlockSpec(memory_space=pltpu.SMEM),
            pl.BlockSpec(memory_space=pl.ANY),
            pl.BlockSpec(memory_space=pl.ANY),
        ],
        out_specs=pl.BlockSpec(memory_space=pltpu.VMEM),
        scratch_shapes=[
            pltpu.VMEM((nk, depth, CHUNK), jnp.bfloat16),
            pltpu.VMEM((nk, depth, CHUNK), jnp.int32),
            pltpu.VMEM((nsamp, nk, 8, CHUNK), jnp.float32),
            pltpu.VMEM((4, 2, width, depth), jnp.bfloat16),
            pltpu.VMEM((nk, rows, CHUNK), jnp.float32),
            coded(4 * npiece, ngrp - 1, rows // 2),
            coded(4 * npiece, ngrp - 1, rows // 2),
            coded(nk, ngrp - 1, rows // 2),
            coded(nk, ngrp - 1, rows // 2),
            coded(nk, rows // 2),
            coded(nk, rows // 2),
            dma((nk,)),
            dma((nk,)),
            dma((nsamp - 1, nk)),
            dma((nsamp - 1, nk)),
            dma((4, npiece)),
            dma((4, npiece)),
            dma((4, npiece)),
            dma((4, npiece)),
            dma((4 * npiece, ngrp - 1)),
            dma((4 * npiece, ngrp - 1)),
            dma((nk, ngrp - 1)),
            dma((nk, ngrp - 1)),
            dma((nk,)),
            dma((nk,)),
        ],
        compiler_params=pltpu.CompilerParams(
            collective_id=0, has_side_effects=True, vmem_limit_bytes=59000 * 1024
        ),
    )(band, dosage, observed)


def solution(mesh):
    return jax.shard_map(
        functools.partial(on_device, mesh.shape["snp"], mesh.shape["samp"]),
        mesh=mesh,
        in_specs=(P("samp", "snp"), P("samp", "snp"), P()),
        out_specs=P(("snp", "samp"), None),
        check_vma=False,
    )
```
